128 devices in a mesh: cluster: 16 (over y, x), kshard: 8 (over z, core).
Axes of the slice: x: 4, y: 4, z: 4, core: 2. Of those that a mesh axis runs over, the one named last changes fastest.
Arguments:
- queries: bfloat16 [8192, 768], P('cluster', 'kshard'), may hold values from -24 to 24
- probes: int32 [64, 4], P('cluster'), may hold values from 0 to 15, all different within a row; in each aligned block of 4 rows (0 to 3, 4 to 7, ...) at most 2 rows name the same one
- key_rows: bfloat16 [16, 16384, 768], P('cluster', 'kshard'), may hold values from -8 to 8
- value_rows: bfloat16 [16, 16384, 768], P('cluster', 'kshard'), may hold values from -6 to 6
- key_scale: float32 [16, 128], P('cluster', 'kshard'), may hold values from 0.25 to 3
- key_tiles: int32 [16], P('cluster'), may hold values from 1 to 128, 1024 in all
Outputs:
- joined: bfloat16 [8192, 768], P('cluster', 'kshard')
The draws below stay inside these ranges and needn't reach their ends.
Inputs may be any that keep to these rules, and one draw needn't show every extreme that they name: `probes`: each row names 4 different clusters; among the tiles of one index of cluster (aligned blocks of 4 tiles) no cluster is named more than 2 times, a bound that some block reaches. `key_tiles`: some cluster has all 128 blocks live.
All inputs are finite; a program needn't handle non-finite values.
Results may differ from the reference program's by a relative error of at most 0.005.
Values may be sent and summed in bfloat16 or wider, within the bound.
A program may use at most 128 MiB of HBM per device.

```python
import math
import jax
import jax.numpy as jnp
import numpy as np
from jax import lax

D = 768
TB = 128
PROBE = 4
KB = 128
TILE_GRP = 4
KEY_DEV = 2048
CLUSTERS = 16
CAP = 2
NTILES = 64
QROWS = 8192
KROWS = 16384
KBLOCKS = 128
N_KSHARD = 8


def draw_queries(key, part):
    drawn = jax.random.normal(jax.random.fold_in(key, 1), (QROWS, D), jnp.float32)
    return jnp.clip(drawn, -24.0, 24.0).astype(jnp.bfloat16)


def draw_key_rows(key, part):
    drawn = jax.random.normal(jax.random.fold_in(key, 4), (CLUSTERS, KROWS, D), jnp.float32)
    return jnp.clip(drawn, -8.0, 8.0).astype(jnp.bfloat16)


def levels(key, extent, split, smallest, top_value):
    gain = 1.0
    for dim, parts in split:
        heights = jax.random.uniform(jax.random.fold_in(jax.random.fold_in(key, 6), dim), (parts,), jnp.float32, smallest / len(split), top_value / len(split))
        gain = gain * jnp.repeat(jnp.exp(heights), extent[dim] // parts).reshape((-1,) + (1,) * (len(extent) - 1 - dim))
    return gain


def split_up(number_of, total, most, slope):
    weights = [(1 << 20) // math.isqrt(rank ** slope) + 1 for rank in range(2, number_of + 1)]
    surplus, holding = total - most - (number_of - 1), [1] * (number_of - 1)
    while surplus > 0:
        free = [i for i in range(number_of - 1) if holding[i] < most]
        mass, remaining = sum([weights[i] for i in free]), surplus
        for i in free:
            more = min(most - holding[i], max(1, remaining * weights[i] // mass), surplus)
            holding[i] = holding[i] + more
            surplus = surplus - more
    return np.array([most] + holding)


def uneven_parts(rng, count, total, bound, slope):
    if count == 2:
        one = jax.random.randint(rng, (), max(1, total - bound), min(bound, total - 1) + 1)
        return jnp.stack([one, total - one])
    sizes = jnp.asarray(split_up(count, total, bound, slope), jnp.int32)
    couples = (count - 1) // 2
    giver, receiver = sizes[1:1 + 2 * couples:2], sizes[2:2 + 2 * couples:2]
    margin = jnp.minimum(giver - 1, bound - receiver)
    moved = jax.random.randint(jax.random.fold_in(rng, 1), (couples,), 0, 1 << 20) % (margin + 1)
    sizes = sizes.at[1:1 + 2 * couples:2].set(giver - moved).at[2:2 + 2 * couples:2].set(receiver + moved)
    return sizes[jax.random.permutation(jax.random.fold_in(rng, 2), count)]


def deal_out(key, own, number, rows, amount, top, bound, skew):
    ranking = jax.random.permutation(key, amount)
    crowded, common = load_shares(amount, rows * top, bound, skew, True), load_shares(amount, rows * top, bound, skew, False)
    places = jnp.arange(amount)

    def named(tallies, rotation):
        used = int((tallies > 0).sum())
        fixed = max(1, used // 4)
        shifted = fixed + (places - fixed + rotation * (used - fixed)) % max(1, amount - fixed)
        return jnp.zeros((amount,), jnp.int32).at[ranking[jnp.where(places < fixed, places, shifted)]].set(jnp.asarray(tallies, jnp.int32))

    tallies = jnp.where(number % 4 == 0, named(crowded, number // 4), named(common, number - number // 4 - 1))
    mixed = jax.random.permutation(jax.random.fold_in(own, 3), amount)
    giver, receiver = mixed[0:amount // 2 * 2:2], mixed[1:amount // 2 * 2:2]
    margin = jnp.minimum(tallies[giver] - 1, bound - tallies[receiver]) // 2
    margin = jnp.where((giver == ranking[0]) | (receiver == ranking[0]) | (tallies[receiver] == 0), 0, jnp.maximum(margin, 0))
    shifted = jax.random.randint(jax.random.fold_in(own, 4), (amount // 2,), 0, 1 << 20) % (margin + 1)
    tallies = tallies.at[giver].add(-shifted).at[receiver].add(shifted)
    items = jnp.searchsorted(jnp.cumsum(tallies), jnp.arange(rows * top), side="right").astype(jnp.int32)
    table = items.reshape(top, rows).T
    table = table[jax.random.permutation(jax.random.fold_in(own, 1), rows)]
    rotation = jax.random.randint(jax.random.fold_in(own, 2), (rows, 1), 0, top)
    return jnp.take_along_axis(table, (jnp.arange(top)[None, :] + rotation) % top, axis=1)


def load_shares(count, total, reach, lean, full):
    weights = [(1 << 20) // math.isqrt(rank ** lean) + 1 for rank in range(1, count + 1)]
    largest = reach if full else min(reach, max(-(-total // count), total * weights[0] // sum(weights)))
    least = 1 if total - largest >= count - 1 else 0
    holding, surplus = [largest] + [least] * (count - 1), total - largest - least * (count - 1)
    while surplus > 0:
        free = [i for i in range(1, count) if holding[i] < largest] or [i for i in range(1, count) if holding[i] < reach]
        pool, left = sum([weights[i] for i in free]), surplus
        for i in free:
            more = min(reach - holding[i], max(1, left * weights[i] // pool), surplus)
            holding[i] = holding[i] + more
            surplus = surplus - more
    return np.array(holding)


def centred(own_key, extent, scale, most, shards=(), kind=jnp.bfloat16):
    entries = scale * jax.random.normal(own_key, extent, jnp.float32)
    if shards:
        entries = entries * levels(own_key, extent, shards, -0.22, 0.18)
    return jnp.clip(entries, -most, most).astype(kind)


def setup_inputs(seed: int = 0) -> dict:
    arg_keys = jax.random.split(jax.random.key(seed), 7)
    queries = draw_queries(jax.random.fold_in(arg_keys[6], 71), 0)
    probes_keys = jax.random.split(jax.random.fold_in(arg_keys[1], 1), NTILES // TILE_GRP)
    probes_turns = jax.random.permutation(jax.random.fold_in(arg_keys[1], 3), NTILES // TILE_GRP)
    probes = jax.vmap(lambda own, number: deal_out(jax.random.fold_in(arg_keys[1], 2), own, number, TILE_GRP, CLUSTERS, PROBE, CAP, 2))(probes_keys, probes_turns).reshape((NTILES, PROBE))
    key_rows = draw_key_rows(jax.random.fold_in(arg_keys[6], 71), 0)
    value_rows = centred(arg_keys[3], (CLUSTERS, KROWS, D), 1.0, 6.0, ((0, 16), (1, 8)))
    key_scale = jnp.clip(jnp.exp(math.log(3.0) - 2.4849066 * jax.random.uniform(arg_keys[4], (CLUSTERS, KBLOCKS), jnp.float32) ** levels(arg_keys[4], (CLUSTERS, KBLOCKS), ((0, 16), (1, 8)), -0.2, 0.2)), 0.25, 3.0)
    key_tiles = uneven_parts(arg_keys[5], CLUSTERS, CLUSTERS * KBLOCKS // 2, KBLOCKS, 2).astype(jnp.int32)
    return dict(queries=queries, probes=probes, key_rows=key_rows, value_rows=value_rows, key_scale=key_scale, key_tiles=key_tiles)


masked_value = -1e+30

def partial_block(query_rows, block_keys, block_values, block_scale, first_row, live_limit):
    products = jnp.dot(query_rows, block_keys.T, preferred_element_type=jnp.float32)
    row_count = products.shape[0]
    scores = (products.reshape(row_count, block_scale.shape[0], -1) * block_scale[None, :, None]).reshape(row_count, -1) * (1.0 / math.sqrt(D))
    key_index = first_row + jnp.arange(block_keys.shape[0], dtype=jnp.int32)
    live_keys = (key_index < live_limit)[None, :]
    masked = jnp.where(live_keys, scores, masked_value)
    row_max = lax.optimization_barrier(jnp.max(masked, axis=1))
    weight = jnp.where(live_keys, jnp.exp(masked - row_max[:, None]), jnp.float32(0.0))
    row_sum = lax.optimization_barrier(jnp.sum(weight, axis=1))
    mixture = jnp.dot(weight.astype(jnp.bfloat16), block_values, preferred_element_type=jnp.float32)
    return (row_max, row_sum, mixture)

def reference(queries, probes, key_rows, value_rows, key_scale, key_tiles):

    def one_probe(query_rows, cluster):
        cluster_keys = lax.dynamic_index_in_dim(key_rows, cluster, 0, keepdims=False).reshape(N_KSHARD, KEY_DEV, D)
        cluster_values = lax.dynamic_index_in_dim(value_rows, cluster, 0, keepdims=False).reshape(N_KSHARD, KEY_DEV, D)
        cluster_scale = lax.dynamic_index_in_dim(key_scale, cluster, 0, keepdims=False).reshape(N_KSHARD, KEY_DEV // KB)
        live_limit = lax.dynamic_index_in_dim(key_tiles, cluster, 0, keepdims=False) * KB
        offsets = jnp.arange(N_KSHARD, dtype=jnp.int32) * KEY_DEV

        def one_block(pieces):
            return partial_block(query_rows, pieces[0], pieces[1], pieces[2], pieces[3], live_limit)
        row_max, row_sum, mixture = lax.map(one_block, (cluster_keys, cluster_values, cluster_scale, offsets))
        highest = lax.optimization_barrier(jnp.max(row_max, axis=0))
        factor = jnp.exp(row_max - highest[None, :])
        row_total = lax.optimization_barrier(jnp.sum(factor * row_sum, axis=0))
        summed = lax.optimization_barrier(jnp.sum(factor[:, :, None] * mixture, axis=0))
        return (highest, row_total, (summed / row_total[:, None]).astype(jnp.bfloat16))

    def one_tile(tile_index):
        query_rows = lax.dynamic_slice_in_dim(queries, tile_index * TB, TB, 0)
        cluster_ids = lax.dynamic_index_in_dim(probes, tile_index, 0, keepdims=False)
        highest, row_total, answer = lax.map(lambda cluster: one_probe(query_rows, cluster), cluster_ids)
        overall = lax.optimization_barrier(jnp.max(highest, axis=0))
        weight = jnp.exp(highest - overall[None, :]) * row_total
        joined = lax.optimization_barrier(jnp.sum(weight[:, :, None] * answer.astype(jnp.float32), axis=0)) / lax.optimization_barrier(jnp.sum(weight, axis=0))[:, None]
        return joined.astype(jnp.bfloat16)
    joined = lax.map(one_tile, jnp.arange(NTILES, dtype=jnp.int32))
    return joined.reshape(QROWS, D)
```

```python
import math

import jax
import jax.numpy as jnp
from jax import lax
from jax.experimental import pallas as pl
from jax.experimental.pallas import tpu as pltpu
from jax.sharding import PartitionSpec as P

D = 768
TB = 128
KB = 128
PROBE = 4
TILES = 4
CLUSTERS = 16
CAP = 2
SIDE = 4
SLICE = 96
KEYS = 2048
CHUNK = 1024
HALF = SIDE * SLICE
STAT = 16
PAIRS = CLUSTERS // 2
MASKED = -1e30
MESH = pl.DeviceIdType.MESH
BF16, F32 = jnp.bfloat16, jnp.float32

ORDER = (
    ((1, 1), (3, 3)),
    ((1, 3), (3, 1)),
    ((2, 0), (0, 2)),
    ((1, 2), (3, 0)),
    ((3, 2), (1, 0)),
    ((2, 1), (0, 3)),
    ((2, 3), (0, 1)),
    ((2, 2), (0, 0)),
)


def shifted(cluster, dy, dx):
    return lax.rem(cluster // SIDE + dy, SIDE) * SIDE + lax.rem(lax.rem(cluster, SIDE) + dx, SIDE)


def picked(values, index):
    code = sum(v * 4**i for i, v in enumerate(values))
    return lax.rem(lax.shift_right_logical(jnp.int32(code), 2 * index), 4)


def terms(x):
    high = x.astype(BF16).astype(F32)
    rest = x - high
    middle = rest.astype(BF16).astype(F32)
    low = (rest - middle).astype(BF16).astype(F32)
    row = lax.broadcasted_iota(jnp.int32, (STAT, x.shape[1]), 0)
    return jnp.where(
        row == 0, high, jnp.where(row == 1, middle, jnp.where(row == 2, low, 0.0))
    ).astype(BF16)


def whole(stat):
    s = stat.astype(F32)
    return s[0:1] + s[1:2] + s[2:3]


def joined(parts, logs):
    top = logs[0]
    for x in logs[1:]:
        top = jnp.maximum(top, x)
    total, mass = None, None
    for part, x in zip(parts, logs):
        w = jnp.exp2(x - top)
        term = part.astype(F32) * w
        total = term if total is None else total + term
        mass = w if mass is None else mass + w
    return total / mass, top + jnp.log2(mass)


def kernel(
    q_ref, probes_ref, scale_ref, tiles_ref, k_hbm, v_hbm, out_ref,
    wide, q_t, pack, qbuf, keys, vals, vt, raw, gain, bias, qp, s_a, s_b, acc,
    osend, rbuf, xsend, xbuf,
    load_sem, send_sem, p1_sem, p2_sem, kv_sem, ret_sem, x_sem,
):
    c, k = lax.axis_index("cluster"), lax.axis_index("kshard")
    z, core = k // 2, lax.rem(k, 2)
    other = 1 - core
    sibling = (c, 2 * z + other)

    def column(dz):
        return (c, 2 * lax.rem(z + dz, SIDE) + core)

    k_load = pltpu.make_async_copy(k_hbm.at[0], keys.at[core], load_sem.at[0])
    v_load = pltpu.make_async_copy(v_hbm.at[0], vals, load_sem.at[1])
    k_load.start()
    v_load.start()

    barrier = pltpu.get_barrier_semaphore()

    def greet(i, carry):
        d = lax.rem(2 * c + core + i, 2 * CLUSTERS)
        pl.semaphore_signal(
            barrier, inc=1, device_id=(d // 2, 2 * z + lax.rem(d, 2)), device_id_type=MESH
        )
        return carry

    lax.fori_loop(1, 2 * CLUSTERS, greet, 0)
    for dz in range(1, SIDE):
        pl.semaphore_signal(barrier, inc=1, device_id=column(dz), device_id_type=MESH)

    wide[...] = jnp.zeros_like(wide)
    wide[:, 0:SLICE] = q_ref[...].astype(F32)
    for t in range(TILES):
        q_t[t] = wide[t * TB : (t + 1) * TB, :].T[0:SLICE].astype(BF16)

    def fill(cc, carry):
        seen, first, second = jnp.int32(0), jnp.int32(0), jnp.int32(0)
        for t in range(TILES):
            hit = jnp.int32(0)
            for p in range(PROBE):
                hit = hit + jnp.where(probes_ref[t, p] == cc, 1, 0)
            first = first + t * hit * jnp.where(seen == 0, 1, 0)
            second = second + t * hit * jnp.where(seen == 1, 1, 0)
            seen = seen + hit
        pack[cc, 0] = q_t[first]
        pack[cc, 1] = q_t[second]
        return carry

    lax.fori_loop(0, CLUSTERS, fill, 0)

    for b in range(KEYS // KB):
        raw[core, b : b + 1, :] = jnp.full((1, 2 * TB), scale_ref[0, b], F32)

    pl.semaphore_wait(barrier, 2 * CLUSTERS - 1 + SIDE - 1)

    for i in range(CLUSTERS):
        dy, dx = ORDER[i // 2][i % 2]
        cc = shifted(c, dy, dx)
        for s in range(CAP):
            remote = pltpu.make_async_remote_copy(
                src_ref=pack.at[cc, s], dst_ref=qbuf.at[i, k],
                send_sem=send_sem.at[0], recv_sem=p1_sem.at[i],
                device_id=(cc, 2 * z + s), device_id_type=MESH,
            )
            if dy == 0 and dx == 0:
                @pl.when(core == s)
                def _():
                    pltpu.make_async_copy(pack.at[cc, s], qbuf.at[i, k], p1_sem.at[i]).start()

                @pl.when(core != s)
                def _():
                    remote.start()
            else:
                remote.start()

    k_send = pltpu.make_async_remote_copy(
        src_ref=k_hbm.at[0], dst_ref=keys.at[core], send_sem=kv_sem.at[0],
        recv_sem=kv_sem.at[1], device_id=sibling, device_id_type=MESH,
    )
    k_send.start()
    raw_send = pltpu.make_async_remote_copy(
        src_ref=raw.at[core], dst_ref=raw.at[core], send_sem=kv_sem.at[2],
        recv_sem=kv_sem.at[3], device_id=sibling, device_id_type=MESH,
    )
    raw_send.start()

    v_load.wait()

    def turn(b, carry):
        rows = pl.ds(pl.multiple_of(b * 256, 256), 256)
        vt[core, :, rows] = vals[rows, :].T
        return carry

    lax.fori_loop(0, KEYS // 256, turn, 0)

    def relay(i):
        mine = qbuf.at[i, pl.ds(2 * z, 2)]
        pltpu.make_async_copy(mine, mine, p1_sem.at[i]).wait()
        for dz in (1, 3, 2):
            pltpu.make_async_remote_copy(
                src_ref=mine, dst_ref=mine, send_sem=send_sem.at[1],
                recv_sem=p2_sem.at[i], device_id=column(dz), device_id_type=MESH,
            ).start()

    relay(0)
    relay(1)
    v_send = pltpu.make_async_remote_copy(
        src_ref=vt.at[core], dst_ref=vt.at[core], send_sem=kv_sem.at[4],
        recv_sem=kv_sem.at[5], device_id=sibling, device_id_type=MESH,
    )
    v_send.start()
    relay(2)
    relay(3)

    k_load.wait()
    raw_send.wait()
    block = z * (2 * KEYS // KB) + lax.broadcasted_iota(jnp.int32, (2 * KEYS // KB, 2 * TB), 0)
    live = block < tiles_ref[0]
    flat = raw[...].reshape(2 * KEYS // KB, 2 * TB)
    gain[...] = jnp.where(live, flat * (math.log2(math.e) / math.sqrt(D)), 0.0)
    bias[...] = jnp.where(live, 0.0, MASKED)
    k_send.wait()
    v_send.wait()

    parts = [(h, j) for h in range(2) for j in range(KEYS // CHUNK)]

    def scored(part, s_ref):
        h, j = part
        s = jnp.dot(
            keys[h, j * CHUNK : (j + 1) * CHUNK, :], qp[...], preferred_element_type=F32
        )
        top = None
        for b in range(CHUNK // KB):
            row = (h * KEYS + j * CHUNK) // KB + b
            x = s[b * KB : (b + 1) * KB] * gain[row : row + 1, :] + bias[row : row + 1, :]
            s_ref[b * KB : (b + 1) * KB, :] = x
            high = jnp.max(x, axis=0, keepdims=True)
            top = high if top is None else jnp.maximum(top, high)
        return top

    def visit(pair, carry):
        @pl.when(pair < PAIRS - 2)
        def _():
            relay(2 * pair + 4)
            relay(2 * pair + 5)

        for u in range(2):
            i = 2 * pair + u
            rest = qbuf.at[i, pl.ds(0, 6)]
            pltpu.make_async_copy(rest, rest, p2_sem.at[i]).wait()
            qp[:, u * TB : (u + 1) * TB] = qbuf[i].reshape(D, TB)

        buffers = (s_a, s_b)
        top = scored(parts[0], buffers[0])
        best, mass = None, None
        for n, (h, j) in enumerate(parts):
            if n + 1 < len(parts):
                next_top = scored(parts[n + 1], buffers[(n + 1) % 2])
            now = top if best is None else jnp.maximum(best, top)
            weight = jnp.exp2(buffers[n % 2][...] - now)
            row_sum = jnp.sum(weight, axis=0, keepdims=True)
            mixture = jnp.dot(
                vt[h, :, j * CHUNK : (j + 1) * CHUNK], weight.astype(BF16),
                preferred_element_type=F32,
            )
            if best is None:
                acc[...] = mixture
                mass = row_sum
            else:
                fade = jnp.exp2(best - now)
                acc[...] = acc[...] * fade + mixture
                mass = mass * fade + row_sum
            best = now
            if n + 1 < len(parts):
                top = next_top

        answer = (acc[...] * (1.0 / mass)).astype(BF16)
        logs = terms(best + jnp.log2(mass))
        for u in range(2):
            i = 2 * pair + u
            lanes = slice(u * TB, (u + 1) * TB)
            for half in range(2):
                for part in range(SIDE):
                    first = (2 * part + half) * SLICE
                    osend[i, half, part * SLICE : (part + 1) * SLICE, :] = answer[
                        first : first + SLICE, lanes
                    ]
                osend[i, half, HALF : HALF + STAT, :] = logs[:, lanes]
        for u in range(2):
            i = 2 * pair + u
            dy = picked([(SIDE - ORDER[n][u][0]) % SIDE for n in range(PAIRS)], pair)
            dx = picked([(SIDE - ORDER[n][u][1]) % SIDE for n in range(PAIRS)], pair)
            g = shifted(c, dy, dx)
            for half in range(2):
                here = jnp.logical_and(g == c, core == half)
                source, target = osend.at[i, half], rbuf.at[CAP * c + core]

                @pl.when(here)
                def _():
                    pltpu.make_async_copy(source, target, ret_sem).start()

                @pl.when(jnp.logical_not(here))
                def _():
                    pltpu.make_async_remote_copy(
                        src_ref=source, dst_ref=target, send_sem=send_sem.at[2],
                        recv_sem=ret_sem, device_id=(g, 2 * z + half), device_id_type=MESH,
                    ).start()

        return carry

    lax.fori_loop(0, PAIRS, visit, 0)

    pltpu.make_async_copy(rbuf, rbuf, ret_sem).wait()

    for t in range(TILES):
        found = []
        for p in range(PROBE):
            cc = probes_ref[t, p]
            slot = jnp.int32(0)
            for before in range(t):
                for other_p in range(PROBE):
                    slot = slot + jnp.where(probes_ref[before, other_p] == cc, 1, 0)
            found.append(CAP * cc + slot)
        logs = [whole(rbuf[f, HALF : HALF + STAT, :]) for f in found]
        total, log = joined([rbuf[f, 0:HALF, :] for f in found], logs)
        stat = terms(log)
        for part in range(SIDE):
            xsend[part, t, 0:SLICE, :] = total[part * SLICE : (part + 1) * SLICE].astype(BF16)
            xsend[part, t, SLICE : SLICE + STAT, :] = stat

    for dz in (2, 1, 3):
        pltpu.make_async_remote_copy(
            src_ref=xsend.at[lax.rem(z + dz, SIDE)], dst_ref=xbuf.at[z],
            send_sem=send_sem.at[3], recv_sem=x_sem, device_id=column(dz), device_id_type=MESH,
        ).start()
    xbuf[z] = xsend[z]
    pltpu.make_async_copy(xsend.at[pl.ds(0, 3)], xsend.at[pl.ds(0, 3)], x_sem).wait()

    for t in range(TILES):
        logs = [whole(xbuf[n, t, SLICE : SLICE + STAT, :]) for n in range(SIDE)]
        total, _ = joined([xbuf[n, t, 0:SLICE, :] for n in range(SIDE)], logs)
        tall = jnp.concatenate([total, jnp.zeros((TB - SLICE, TB), F32)], axis=0)
        out_ref[t * TB : (t + 1) * TB, :] = tall.T[:, 0:SLICE].astype(BF16)

    flat_pack = pack.at[pl.ds(0, 15)]
    pltpu.make_async_copy(flat_pack, flat_pack, send_sem.at[0]).wait()
    pltpu.make_async_copy(pack.at[0, 0], pack.at[0, 0], send_sem.at[0]).wait()
    relayed = qbuf.at[pl.ds(0, 12)]
    pltpu.make_async_copy(relayed, relayed, send_sem.at[1]).wait()
    most = osend.at[pl.ds(0, 15)]
    pltpu.make_async_copy(most, most, send_sem.at[2]).wait()
    pltpu.make_async_copy(osend.at[0, 0], osend.at[0, 0], send_sem.at[2]).wait()
    pltpu.make_async_copy(xsend.at[pl.ds(0, 3)], xsend.at[pl.ds(0, 3)], send_sem.at[3]).wait()


def shards(queries, probes, key_rows, value_rows, key_scale, key_tiles):
    vmem = pl.BlockSpec(memory_space=pltpu.VMEM)
    smem = pl.BlockSpec(memory_space=pltpu.SMEM)
    hbm = pl.BlockSpec(memory_space=pl.ANY)
    dma = pltpu.SemaphoreType.DMA
    return pl.pallas_call(
        kernel,
        out_shape=jax.ShapeDtypeStruct((TILES * TB, SLICE), BF16),
        in_specs=[vmem, smem, smem, smem, hbm, hbm],
        out_specs=vmem,
        scratch_shapes=[
            pltpu.VMEM((TILES * TB, TB), F32),
            pltpu.VMEM((TILES, SLICE, TB), BF16),
            pltpu.VMEM((CLUSTERS, CAP, SLICE, TB), BF16),
            pltpu.VMEM((CLUSTERS, 2 * SIDE, SLICE, TB), BF16),
            pltpu.VMEM((2, KEYS, D), BF16),
            pltpu.VMEM((KEYS, D), BF16),
            pltpu.VMEM((2, D, KEYS), BF16),
            pltpu.VMEM((2, KEYS // KB, 2 * TB), F32),
            pltpu.VMEM((2 * KEYS // KB, 2 * TB), F32),
            pltpu.VMEM((2 * KEYS // KB, 2 * TB), F32),
            pltpu.VMEM((D, 2 * TB), BF16),
            pltpu.VMEM((CHUNK, 2 * TB), F32),
            pltpu.VMEM((CHUNK, 2 * TB), F32),
            pltpu.VMEM((D, 2 * TB), F32),
            pltpu.VMEM((CLUSTERS, 2, HALF + STAT, TB), BF16),
            pltpu.VMEM((CAP * CLUSTERS, HALF + STAT, TB), BF16),
            pltpu.VMEM((SIDE, TILES, SLICE + STAT, TB), BF16),
            pltpu.VMEM((SIDE, TILES, SLICE + STAT, TB), BF16),
            dma((2,)),
            dma((4,)),
            dma((CLUSTERS,)),
            dma((CLUSTERS,)),
            dma((6,)),
            dma,
            dma,
        ],
        compiler_params=pltpu.CompilerParams(
            collective_id=0, has_side_effects=True, vmem_limit_bytes=60 * 2**20
        ),
    )(queries, probes, key_scale, key_tiles, key_rows, value_rows)


def solution(mesh):
    return jax.shard_map(
        shards,
        mesh=mesh,
        in_specs=(
            P("cluster", "kshard"),
            P("cluster", None),
            P("cluster", "kshard", None),
            P("cluster", "kshard", None),
            P("cluster", "kshard"),
            P("cluster"),
        ),
        out_specs=P("cluster", "kshard"),
        check_vma=False,
    )
```

```python
import math

import jax
import jax.numpy as jnp
from jax import lax
from jax.experimental import pallas as pl
from jax.experimental.pallas import tpu as pltpu
from jax.sharding import PartitionSpec as P

D = 768
TB = 128
KB = 128
PROBE = 4
TILES = 4
CLUSTERS = 16
CAP = 2
SIDE = 4
SLICE = 96
KEYS = 2048
CHUNK = 256
HALF = SIDE * SLICE
STAT = 16
PAIRS = CLUSTERS // 2
FAR = 2
NEAR = PAIRS - FAR
WIDE = 2 * SLICE
MASKED = -1e30
MESH = pl.DeviceIdType.MESH
BF16, F32 = jnp.bfloat16, jnp.float32

ORDER = (
    ((1, 1), (3, 3)),
    ((1, 3), (3, 1)),
    ((1, 2), (3, 0)),
    ((3, 2), (1, 0)),
    ((2, 1), (0, 3)),
    ((2, 3), (0, 1)),
    ((2, 2), (0, 2)),
    ((2, 0), (0, 0)),
)


def shifted(cluster, dy, dx):
    return lax.rem(cluster // SIDE + dy, SIDE) * SIDE + lax.rem(lax.rem(cluster, SIDE) + dx, SIDE)


def picked(values, index):
    code = sum(v * 4**i for i, v in enumerate(values))
    return lax.rem(lax.shift_right_logical(jnp.int32(code), 2 * index), 4)


def terms(x):
    high = x.astype(BF16).astype(F32)
    rest = x - high
    middle = rest.astype(BF16).astype(F32)
    low = (rest - middle).astype(BF16).astype(F32)
    row = lax.broadcasted_iota(jnp.int32, (STAT, x.shape[1]), 0)
    return jnp.where(
        row == 0, high, jnp.where(row == 1, middle, jnp.where(row == 2, low, 0.0))
    ).astype(BF16)


def whole(stat):
    s = stat.astype(F32)
    return s[0:1] + s[1:2] + s[2:3]


def joined(parts, logs):
    top = logs[0]
    for x in logs[1:]:
        top = jnp.maximum(top, x)
    total, mass = None, None
    for part, x in zip(parts, logs):
        w = jnp.exp2(x - top)
        term = part.astype(F32) * w
        total = term if total is None else total + term
        mass = w if mass is None else mass + w
    return total / mass, top + jnp.log2(mass)


def kernel(
    q_ref, probes_ref, scale_ref, tiles_ref, k_hbm, v_hbm, out_ref,
    q_t, pack, qbuf, keys, vals, vt, raw, gain, bias, qp, s_a, s_b, acc, answer, logs,
    osend, rbuf, xsend, xbuf, zsend, zbuf, fsend, fbuf,
    load_sem, pack_sem, send_sem, p1_sem, left_sem, right_sem, far_sem, kv_sem, ret_sem, x_sem, z_sem, f_sem,
):
    c, k = lax.axis_index("cluster"), lax.axis_index("kshard")
    z, core = k // 2, lax.rem(k, 2)
    other = 1 - core
    sibling = (c, 2 * z + other)

    def column(dz):
        return (c, 2 * lax.rem(z + dz, SIDE) + core)

    k_load = pltpu.make_async_copy(k_hbm.at[0], keys.at[core], load_sem.at[0])
    v_load = pltpu.make_async_copy(v_hbm.at[0], vals, load_sem.at[1])
    k_load.start()
    v_load.start()

    barrier = pltpu.get_barrier_semaphore()

    def greet(i, carry):
        d = lax.rem(2 * c + core + i, 2 * CLUSTERS)
        pl.semaphore_signal(
            barrier, inc=1, device_id=(d // 2, 2 * z + lax.rem(d, 2)), device_id_type=MESH
        )
        return carry

    lax.fori_loop(1, 2 * CLUSTERS, greet, 0)
    for dz in range(1, SIDE):
        pl.semaphore_signal(barrier, inc=1, device_id=column(dz), device_id_type=MESH)

    for t in range(TILES):
        q_t[t] = q_ref[:, t * TB : (t + 1) * TB]

    def fill(cc, carry):
        seen, first, second = jnp.int32(0), jnp.int32(0), jnp.int32(0)
        for t in range(TILES):
            hit = jnp.int32(0)
            for p in range(PROBE):
                hit = hit + jnp.where(probes_ref[t, p] == cc, 1, 0)
            first = first + t * hit * jnp.where(seen == 0, 1, 0)
            second = second + t * hit * jnp.where(seen == 1, 1, 0)
            seen = seen + hit
        pack[cc, 0] = q_t[first]
        pack[cc, 1] = q_t[second]
        return carry

    lax.fori_loop(0, CLUSTERS, fill, 0)

    for b in range(KEYS // KB):
        raw[core, b : b + 1, :] = jnp.full((1, 2 * TB), scale_ref[0, b], F32)

    far_clusters = [shifted(c, *ORDER[NEAR + n // 2][n % 2]) for n in range(2 * FAR)]
    stand_in = CAP * shifted(c, *ORDER[0][0])
    places = []
    for t in range(TILES):
        row = []
        for p in range(PROBE):
            cc = probes_ref[t, p]
            slot = jnp.int32(0)
            for before in range(t):
                for other_p in range(PROBE):
                    slot = slot + jnp.where(probes_ref[before, other_p] == cc, 1, 0)
            slot = jnp.minimum(slot, CAP - 1)
            far, number = jnp.int32(0), jnp.int32(0)
            for n, f in enumerate(far_clusters):
                hit = jnp.where(f == cc, 1, 0)
                far, number = far + hit, number + n * hit
            row.append((
                jnp.where(far == 1, stand_in, CAP * cc + slot),
                CAP * number + slot,
                jnp.where(far == 1, MASKED, 0.0),
                jnp.where(far == 1, 0.0, MASKED),
            ))
        places.append(row)

    pl.semaphore_wait(barrier, 2 * CLUSTERS - 1 + SIDE - 1)

    for i in range(CLUSTERS):
        dy, dx = ORDER[i // 2][i % 2]
        cc = shifted(c, dy, dx)
        for s in range(CAP):
            remote = pltpu.make_async_remote_copy(
                src_ref=pack.at[cc, s], dst_ref=qbuf.at[i, k],
                send_sem=pack_sem, recv_sem=p1_sem.at[i],
                device_id=(cc, 2 * z + s), device_id_type=MESH,
            )
            if dy == 0 and dx == 0:
                @pl.when(core == s)
                def _():
                    pltpu.make_async_copy(pack.at[cc, s], qbuf.at[i, k], p1_sem.at[i]).start()

                @pl.when(core != s)
                def _():
                    remote.start()
            else:
                remote.start()

    k_send = pltpu.make_async_remote_copy(
        src_ref=k_hbm.at[0], dst_ref=keys.at[core], send_sem=kv_sem.at[0],
        recv_sem=kv_sem.at[1], device_id=sibling, device_id_type=MESH,
    )
    k_send.start()
    raw_send = pltpu.make_async_remote_copy(
        src_ref=raw.at[core], dst_ref=raw.at[core], send_sem=kv_sem.at[2],
        recv_sem=kv_sem.at[3], device_id=sibling, device_id_type=MESH,
    )
    raw_send.start()

    def turn(b, carry):
        rows = pl.ds(pl.multiple_of(b * 256, 256), 256)
        vt[core, :, rows] = vals[rows, :].T
        return carry

    left, right = lax.rem(z + SIDE - 1, SIDE), lax.rem(z + 1, SIDE)

    def spread(i):
        mine = qbuf.at[i, pl.ds(2 * z, 2)]
        pltpu.make_async_copy(mine, mine, p1_sem.at[i]).wait()
        for arrival, target in ((left_sem, right), (right_sem, left)):
            pltpu.make_async_remote_copy(
                src_ref=mine, dst_ref=mine, send_sem=send_sem.at[1], recv_sem=arrival.at[i],
                device_id=(c, 2 * target + core), device_id_type=MESH,
            ).start()

    def forward(i):
        for arrival, source, target, n in ((left_sem, left, right, 0), (right_sem, right, left, 1)):
            both = qbuf.at[i, pl.ds(2 * source, 2)]
            pltpu.make_async_copy(both, both, arrival.at[i]).wait()
            one = qbuf.at[i, 2 * source + n]
            pltpu.make_async_remote_copy(
                src_ref=one, dst_ref=one, send_sem=send_sem.at[1], recv_sem=far_sem.at[i],
                device_id=(c, 2 * target + core), device_id_type=MESH,
            ).start()

    for i in range(4):
        spread(i)
    v_load.wait()
    lax.fori_loop(0, KEYS // 256, turn, 0)
    v_send = pltpu.make_async_remote_copy(
        src_ref=vt.at[core], dst_ref=vt.at[core], send_sem=kv_sem.at[4],
        recv_sem=kv_sem.at[5], device_id=sibling, device_id_type=MESH,
    )
    v_send.start()
    for i in range(4, 6):
        spread(i)
    for i in range(2):
        forward(i)

    k_load.wait()
    raw_send.wait()
    for h in range(2):
        block = lax.broadcasted_iota(jnp.int32, (KEYS // KB, 2 * TB), 0)
        live = block + (2 * z + h) * (KEYS // KB) < tiles_ref[0]
        gain[h] = jnp.where(live, raw[h] * (math.log2(math.e) / math.sqrt(D)), 0.0)
        bias[h] = jnp.where(live, 0.0, MASKED)

    parts = [(h, j) for h in (core, other) for j in range(KEYS // CHUNK)]

    def scored(part, s_ref):
        h, j = part
        s = jnp.dot(
            keys[h, j * CHUNK : (j + 1) * CHUNK, :], qp[...], preferred_element_type=F32
        )
        top = None
        for b in range(CHUNK // KB):
            row = slice(j * CHUNK // KB + b, j * CHUNK // KB + b + 1)
            x = s[b * KB : (b + 1) * KB] * gain[h, row, :] + bias[h, row, :]
            s_ref[b * KB : (b + 1) * KB, :] = x
            high = jnp.max(x, axis=0, keepdims=True)
            top = high if top is None else jnp.maximum(top, high)
        return top

    def visit(pair, carry):
        @pl.when(pair < PAIRS - 1)
        def _():
            for u in range(2):
                forward(2 * pair + 2 + u)

        @pl.when(pair < PAIRS - 3)
        def _():
            for u in range(2):
                spread(2 * pair + 6 + u)

        for u in range(2):
            i = 2 * pair + u
            rest = qbuf.at[i, pl.ds(0, 2)]
            pltpu.make_async_copy(rest, rest, far_sem.at[i]).wait()
            qp[:, u * TB : (u + 1) * TB] = qbuf[i].reshape(D, TB)

        buffers = (s_a, s_b)
        top = scored(parts[0], buffers[0])
        best, mass = None, None
        for n, (h, j) in enumerate(parts):
            if n + 1 == len(parts) // 2:

                @pl.when(pair == 0)
                def _():
                    k_send.wait()
                    v_send.wait()

            if n + 1 < len(parts):
                next_top = scored(parts[n + 1], buffers[(n + 1) % 2])
            now = top if best is None else jnp.maximum(best, top)
            weight = jnp.exp2(buffers[n % 2][...] - now)
            row_sum = jnp.sum(weight, axis=0, keepdims=True)
            mixture = jnp.dot(
                vt[h, :, j * CHUNK : (j + 1) * CHUNK], weight.astype(BF16),
                preferred_element_type=F32,
            )
            if best is None:
                acc[...] = mixture
                mass = row_sum
            else:
                fade = jnp.exp2(best - now)
                acc[...] = acc[...] * fade + mixture
                mass = mass * fade + row_sum
            best = now
            if n + 1 < len(parts):
                top = next_top

        answer[...] = (acc[...] * (1.0 / mass)).astype(BF16)
        logs[...] = terms(best + jnp.log2(mass))

        @pl.when(pair < NEAR)
        def _():
            for u in range(2):
                i = 2 * pair + u
                lanes = slice(u * TB, (u + 1) * TB)
                for half in range(2):
                    for part in range(SIDE):
                        first = (2 * part + half) * SLICE
                        osend[i, half, part * SLICE : (part + 1) * SLICE, :] = answer[
                            first : first + SLICE, lanes
                        ]
                    osend[i, half, HALF : HALF + STAT, :] = logs[:, lanes]
            for u in range(2):
                i = 2 * pair + u
                dy = picked([(SIDE - ORDER[n][u][0]) % SIDE for n in range(PAIRS)], pair)
                dx = picked([(SIDE - ORDER[n][u][1]) % SIDE for n in range(PAIRS)], pair)
                for half in range(2):
                    pltpu.make_async_remote_copy(
                        src_ref=osend.at[i, half], dst_ref=rbuf.at[CAP * c + core],
                        send_sem=send_sem.at[2], recv_sem=ret_sem,
                        device_id=(shifted(c, dy, dx), 2 * z + half), device_id_type=MESH,
                    ).start()

        @pl.when(pair >= NEAR)
        def _():
            for u in range(2):
                n = 2 * (pair - NEAR) + u
                lanes = slice(u * TB, (u + 1) * TB)
                for part in range(SIDE):
                    zsend[n, part, 0:WIDE, :] = answer[part * WIDE : (part + 1) * WIDE, lanes]
                    zsend[n, part, WIDE : WIDE + STAT, :] = logs[:, lanes]
            for u in range(2):
                n = 2 * (pair - NEAR) + u
                for dz in (2, 1, 3):
                    pltpu.make_async_remote_copy(
                        src_ref=zsend.at[n, lax.rem(z + dz, SIDE)], dst_ref=zbuf.at[n, z],
                        send_sem=send_sem.at[0], recv_sem=z_sem.at[n], device_id=column(dz),
                        device_id_type=MESH,
                    ).start()

        return carry

    lax.fori_loop(0, PAIRS, visit, 0)

    def settle(n):
        three = zsend.at[n, pl.ds(0, 3)]
        pltpu.make_async_copy(three, three, z_sem.at[n]).wait()
        found = [zsend[n, z]] + [zbuf[n, lax.rem(z + dz, SIDE)] for dz in range(1, SIDE)]
        total, log = joined([x[0:WIDE] for x in found], [whole(x[WIDE : WIDE + STAT]) for x in found])
        stat = terms(log)
        dy, dx = ORDER[NEAR + n // 2][n % 2]
        g = shifted(c, (SIDE - dy) % SIDE, (SIDE - dx) % SIDE)
        for half in range(2):
            fsend[2 * n + half, 0:SLICE, :] = total[half * SLICE : (half + 1) * SLICE].astype(BF16)
            fsend[2 * n + half, SLICE : SLICE + STAT, :] = stat
        for half in range(2):
            source, target = fsend.at[2 * n + half], fbuf.at[CAP * n + core]
            remote = pltpu.make_async_remote_copy(
                src_ref=source, dst_ref=target, send_sem=send_sem.at[4], recv_sem=f_sem,
                device_id=(g, 2 * z + half), device_id_type=MESH,
            )
            if dy == 0 and dx == 0:

                @pl.when(core == half)
                def _():
                    pltpu.make_async_copy(source, target, f_sem).start()

                @pl.when(core != half)
                def _():
                    remote.start()
            else:
                remote.start()

    settle(0)
    settle(1)

    arrived = rbuf.at[pl.ds(0, 4 * NEAR)]
    pltpu.make_async_copy(arrived, arrived, ret_sem).wait()
    for t in range(TILES):
        logs_t = [whole(rbuf[f, HALF : HALF + STAT, :]) + m for f, _, m, _ in places[t]]
        total, log = joined([rbuf[f, 0:HALF, :] for f, _, _, _ in places[t]], logs_t)
        stat = terms(log)
        for part in range(SIDE):
            xsend[part, t, 0:SLICE, :] = total[part * SLICE : (part + 1) * SLICE].astype(BF16)
            xsend[part, t, SLICE : SLICE + STAT, :] = stat
        for dz in (2, 1, 3):
            pltpu.make_async_remote_copy(
                src_ref=xsend.at[lax.rem(z + dz, SIDE), t], dst_ref=xbuf.at[z, t],
                send_sem=send_sem.at[3], recv_sem=x_sem.at[t], device_id=column(dz),
                device_id_type=MESH,
            ).start()
        xbuf[z, t] = xsend[z, t]

    settle(2)
    settle(3)

    pltpu.make_async_copy(fbuf, fbuf, f_sem).wait()
    for t in range(TILES):
        three = xsend.at[pl.ds(0, 3), t]
        pltpu.make_async_copy(three, three, x_sem.at[t]).wait()
        found = [xbuf[n, t] for n in range(SIDE)]
        logs_t = [whole(x[SLICE : SLICE + STAT]) for x in found]
        for _, f, _, m in places[t]:
            found.append(fbuf[f])
            logs_t.append(whole(found[-1][SLICE : SLICE + STAT]) + m)
        total, _ = joined([x[0:SLICE] for x in found], logs_t)
        out_ref[:, t * TB : (t + 1) * TB] = total.astype(BF16)

    flat_pack = pack.at[pl.ds(0, 15)]
    pltpu.make_async_copy(flat_pack, flat_pack, pack_sem).wait()
    pltpu.make_async_copy(pack.at[0, 0], pack.at[0, 0], pack_sem).wait()
    relayed = qbuf.at[pl.ds(0, 12)]
    pltpu.make_async_copy(relayed, relayed, send_sem.at[1]).wait()
    pltpu.make_async_copy(osend, osend, send_sem.at[2]).wait()
    three = zsend.at[pl.ds(0, 3)]
    pltpu.make_async_copy(three, three, send_sem.at[0]).wait()
    pltpu.make_async_copy(xsend.at[pl.ds(0, 3)], xsend.at[pl.ds(0, 3)], send_sem.at[3]).wait()
    seven = fsend.at[pl.ds(0, 7)]
    pltpu.make_async_copy(seven, seven, send_sem.at[4]).wait()


def shards(queries, probes, key_rows, value_rows, key_scale, key_tiles):
    vmem = pl.BlockSpec(memory_space=pltpu.VMEM)
    smem = pl.BlockSpec(memory_space=pltpu.SMEM)
    hbm = pl.BlockSpec(memory_space=pl.ANY)
    dma = pltpu.SemaphoreType.DMA
    return pl.pallas_call(
        kernel,
        out_shape=jax.ShapeDtypeStruct((SLICE, TILES * TB), BF16),
        in_specs=[vmem, smem, smem, smem, hbm, hbm],
        out_specs=vmem,
        scratch_shapes=[
            pltpu.VMEM((TILES, SLICE, TB), BF16),
            pltpu.VMEM((CLUSTERS, CAP, SLICE, TB), BF16),
            pltpu.VMEM((CLUSTERS, 2 * SIDE, SLICE, TB), BF16),
            pltpu.VMEM((2, KEYS, D), BF16),
            pltpu.VMEM((KEYS, D), BF16),
            pltpu.VMEM((2, D, KEYS), BF16),
            pltpu.VMEM((2, KEYS // KB, 2 * TB), F32),
            pltpu.VMEM((2, KEYS // KB, 2 * TB), F32),
            pltpu.VMEM((2, KEYS // KB, 2 * TB), F32),
            pltpu.VMEM((D, 2 * TB), BF16),
            pltpu.VMEM((CHUNK, 2 * TB), F32),
            pltpu.VMEM((CHUNK, 2 * TB), F32),
            pltpu.VMEM((D, 2 * TB), F32),
            pltpu.VMEM((D, 2 * TB), BF16),
            pltpu.VMEM((STAT, 2 * TB), BF16),
            pltpu.VMEM((2 * NEAR, 2, HALF + STAT, TB), BF16),
            pltpu.VMEM((CAP * CLUSTERS, HALF + STAT, TB), BF16),
            pltpu.VMEM((SIDE, TILES, SLICE + STAT, TB), BF16),
            pltpu.VMEM((SIDE, TILES, SLICE + STAT, TB), BF16),
            pltpu.VMEM((2 * FAR, SIDE, WIDE + STAT, TB), BF16),
            pltpu.VMEM((2 * FAR, SIDE, WIDE + STAT, TB), BF16),
            pltpu.VMEM((4 * FAR, SLICE + STAT, TB), BF16),
            pltpu.VMEM((4 * FAR, SLICE + STAT, TB), BF16),
            dma((2,)),
            dma,
            dma((5,)),
            dma((CLUSTERS,)),
            dma((CLUSTERS,)),
            dma((CLUSTERS,)),
            dma((CLUSTERS,)),
            dma((6,)),
            dma,
            dma((TILES,)),
            dma((2 * FAR,)),
            dma,
        ],
        compiler_params=pltpu.CompilerParams(
            collective_id=0, has_side_effects=True, vmem_limit_bytes=60 * 2**20
        ),
    )(queries.T, probes, key_scale, key_tiles, key_rows, value_rows).T


def solution(mesh):
    return jax.shard_map(
        shards,
        mesh=mesh,
        in_specs=(
            P("cluster", "kshard"),
            P("cluster", None),
            P("cluster", "kshard", None),
            P("cluster", "kshard", None),
            P("cluster", "kshard"),
            P("cluster"),
        ),
        out_specs=P("cluster", "kshard"),
        check_vma=False,
    )
```

```python
import math

import jax
import jax.numpy as jnp
from jax import lax
from jax.experimental import pallas as pl
from jax.experimental.pallas import tpu as pltpu
from jax.sharding import PartitionSpec as P

D = 768
TB = 128
KB = 128
PROBE = 4
TILES = 4
CLUSTERS = 16
CAP = 2
SIDE = 4
SLICE = 96
KEYS = 2048
CHUNK = 256
HALF = SIDE * SLICE
STAT = 16
PAIRS = CLUSTERS // 2
FAR = 2
NEAR = PAIRS - FAR
WIDE = 2 * SLICE
MASKED = -1e30
MESH = pl.DeviceIdType.MESH
BF16, F32 = jnp.bfloat16, jnp.float32

ORDER = (
    ((1, 1), (3, 3)),
    ((1, 3), (3, 1)),
    ((1, 2), (3, 0)),
    ((3, 2), (1, 0)),
    ((2, 1), (0, 3)),
    ((2, 3), (0, 1)),
    ((2, 2), (0, 2)),
    ((2, 0), (0, 0)),
)


def shifted(cluster, dy, dx):
    return lax.rem(cluster // SIDE + dy, SIDE) * SIDE + lax.rem(lax.rem(cluster, SIDE) + dx, SIDE)


def picked(values, index):
    code = sum(v * 4**i for i, v in enumerate(values))
    return lax.rem(lax.shift_right_logical(jnp.int32(code), 2 * index), 4)


def terms(x):
    high = x.astype(BF16).astype(F32)
    rest = x - high
    middle = rest.astype(BF16).astype(F32)
    low = (rest - middle).astype(BF16).astype(F32)
    row = lax.broadcasted_iota(jnp.int32, (STAT, x.shape[1]), 0)
    return jnp.where(
        row == 0, high, jnp.where(row == 1, middle, jnp.where(row == 2, low, 0.0))
    ).astype(BF16)


def whole(stat):
    s = stat.astype(F32)
    return s[0:1] + s[1:2] + s[2:3]


def joined(parts, logs):
    top = logs[0]
    for x in logs[1:]:
        top = jnp.maximum(top, x)
    total, mass = None, None
    for part, x in zip(parts, logs):
        w = jnp.exp2(x - top)
        term = part.astype(F32) * w
        total = term if total is None else total + term
        mass = w if mass is None else mass + w
    return total / mass, top + jnp.log2(mass)


def kernel(
    q_ref, probes_ref, scale_ref, tiles_ref, k_hbm, v_hbm, out_ref,
    q_t, pack, qbuf, keys, vals, vt, raw, gain, bias, qp, s_a, s_b, acc, answer, logs,
    osend, rbuf, xsend, xbuf, zsend, zbuf, fsend, fbuf,
    load_sem, pack_sem, send_sem, p1_sem, left_sem, right_sem, far_sem, kv_sem, ret_sem, x_sem, z_sem, f_sem,
):
    c, k = lax.axis_index("cluster"), lax.axis_index("kshard")
    z, core = k // 2, lax.rem(k, 2)
    other = 1 - core
    sibling = (c, 2 * z + other)

    def column(dz):
        return (c, 2 * lax.rem(z + dz, SIDE) + core)

    k_load = pltpu.make_async_copy(k_hbm.at[0], keys.at[core], load_sem.at[0])
    v_load = pltpu.make_async_copy(v_hbm.at[0], vals, load_sem.at[1])
    k_load.start()
    v_load.start()

    barrier = pltpu.get_barrier_semaphore()

    def greet(i, carry):
        d = lax.rem(2 * c + core + i, 2 * CLUSTERS)
        pl.semaphore_signal(
            barrier, inc=1, device_id=(d // 2, 2 * z + lax.rem(d, 2)), device_id_type=MESH
        )
        return carry

    lax.fori_loop(1, 2 * CLUSTERS, greet, 0)
    for dz in range(1, SIDE):
        pl.semaphore_signal(barrier, inc=1, device_id=column(dz), device_id_type=MESH)

    for t in range(TILES):
        q_t[t] = q_ref[:, t * TB : (t + 1) * TB]

    def fill(cc, carry):
        seen, first, second = jnp.int32(0), jnp.int32(0), jnp.int32(0)
        for t in range(TILES):
            hit = jnp.int32(0)
            for p in range(PROBE):
                hit = hit + jnp.where(probes_ref[t, p] == cc, 1, 0)
            first = first + t * hit * jnp.where(seen == 0, 1, 0)
            second = second + t * hit * jnp.where(seen == 1, 1, 0)
            seen = seen + hit
        pack[cc, 0] = q_t[first]
        pack[cc, 1] = q_t[second]
        return carry

    lax.fori_loop(0, CLUSTERS, fill, 0)

    for b in range(KEYS // KB):
        raw[core, b : b + 1, :] = jnp.full((1, 2 * TB), scale_ref[0, b], F32)

    far_clusters = [shifted(c, *ORDER[NEAR + n // 2][n % 2]) for n in range(2 * FAR)]
    stand_in = CAP * shifted(c, *ORDER[0][0])
    places = []
    for t in range(TILES):
        row = []
        for p in range(PROBE):
            cc = probes_ref[t, p]
            slot = jnp.int32(0)
            for before in range(t):
                for other_p in range(PROBE):
                    slot = slot + jnp.where(probes_ref[before, other_p] == cc, 1, 0)
            slot = jnp.minimum(slot, CAP - 1)
            far, number = jnp.int32(0), jnp.int32(0)
            for n, f in enumerate(far_clusters):
                hit = jnp.where(f == cc, 1, 0)
                far, number = far + hit, number + n * hit
            row.append((
                jnp.where(far == 1, stand_in, CAP * cc + slot),
                CAP * number + slot,
                jnp.where(far == 1, MASKED, 0.0),
                jnp.where(far == 1, 0.0, MASKED),
            ))
        places.append(row)

    pl.semaphore_wait(barrier, 2 * CLUSTERS - 1 + SIDE - 1)

    for i in range(CLUSTERS):
        dy, dx = ORDER[i // 2][i % 2]
        cc = shifted(c, dy, dx)
        for s in range(CAP):
            remote = pltpu.make_async_remote_copy(
                src_ref=pack.at[cc, s], dst_ref=qbuf.at[i, k],
                send_sem=pack_sem, recv_sem=p1_sem.at[i],
                device_id=(cc, 2 * z + s), device_id_type=MESH,
            )
            if dy == 0 and dx == 0:
                @pl.when(core == s)
                def _():
                    pltpu.make_async_copy(pack.at[cc, s], qbuf.at[i, k], p1_sem.at[i]).start()

                @pl.when(core != s)
                def _():
                    remote.start()
            else:
                remote.start()

    k_send = pltpu.make_async_remote_copy(
        src_ref=k_hbm.at[0], dst_ref=keys.at[core], send_sem=kv_sem.at[0],
        recv_sem=kv_sem.at[1], device_id=sibling, device_id_type=MESH,
    )
    k_send.start()
    raw_send = pltpu.make_async_remote_copy(
        src_ref=raw.at[core], dst_ref=raw.at[core], send_sem=kv_sem.at[2],
        recv_sem=kv_sem.at[3], device_id=sibling, device_id_type=MESH,
    )
    raw_send.start()

    def turn(b, carry):
        rows = pl.ds(pl.multiple_of(b * 256, 256), 256)
        vt[core, :, rows] = vals[rows, :].T
        return carry

    left, right = lax.rem(z + SIDE - 1, SIDE), lax.rem(z + 1, SIDE)

    def spread(i):
        mine = qbuf.at[i, pl.ds(2 * z, 2)]
        pltpu.make_async_copy(mine, mine, p1_sem.at[i]).wait()
        for arrival, target in ((left_sem, right), (right_sem, left)):
            pltpu.make_async_remote_copy(
                src_ref=mine, dst_ref=mine, send_sem=send_sem.at[1], recv_sem=arrival.at[i],
                device_id=(c, 2 * target + core), device_id_type=MESH,
            ).start()

    def forward(i):
        for arrival, source, target, n in ((left_sem, left, right, 0), (right_sem, right, left, 1)):
            both = qbuf.at[i, pl.ds(2 * source, 2)]
            pltpu.make_async_copy(both, both, arrival.at[i]).wait()
            one = qbuf.at[i, 2 * source + n]
            pltpu.make_async_remote_copy(
                src_ref=one, dst_ref=one, send_sem=send_sem.at[1], recv_sem=far_sem.at[i],
                device_id=(c, 2 * target + core), device_id_type=MESH,
            ).start()

    for i in range(2):
        spread(i)
    v_load.wait()
    lax.fori_loop(0, KEYS // 256, turn, 0)
    v_send = pltpu.make_async_remote_copy(
        src_ref=vt.at[core], dst_ref=vt.at[core], send_sem=kv_sem.at[4],
        recv_sem=kv_sem.at[5], device_id=sibling, device_id_type=MESH,
    )
    v_send.start()
    for i in range(2):
        forward(i)
    for i in range(2, 6):
        spread(i)

    k_load.wait()
    raw_send.wait()
    for h in range(2):
        block = lax.broadcasted_iota(jnp.int32, (KEYS // KB, 2 * TB), 0)
        live = block + (2 * z + h) * (KEYS // KB) < tiles_ref[0]
        gain[h] = jnp.where(live, raw[h] * (math.log2(math.e) / math.sqrt(D)), 0.0)
        bias[h] = jnp.where(live, 0.0, MASKED)

    parts = [(h, j) for h in (core, other) for j in range(KEYS // CHUNK)]

    def scored(part, s_ref):
        h, j = part
        s = jnp.dot(
            keys[h, j * CHUNK : (j + 1) * CHUNK, :], qp[...], preferred_element_type=F32
        )
        top = None
        for b in range(CHUNK // KB):
            row = slice(j * CHUNK // KB + b, j * CHUNK // KB + b + 1)
            x = s[b * KB : (b + 1) * KB] * gain[h, row, :] + bias[h, row, :]
            s_ref[b * KB : (b + 1) * KB, :] = x
            high = jnp.max(x, axis=0, keepdims=True)
            top = high if top is None else jnp.maximum(top, high)
        return top

    def visit(pair, carry):
        @pl.when(pair < PAIRS - 1)
        def _():
            for u in range(2):
                forward(2 * pair + 2 + u)

        @pl.when(pair < PAIRS - 3)
        def _():
            for u in range(2):
                spread(2 * pair + 6 + u)

        for u in range(2):
            i = 2 * pair + u
            rest = qbuf.at[i, pl.ds(0, 2)]
            pltpu.make_async_copy(rest, rest, far_sem.at[i]).wait()
            qp[:, u * TB : (u + 1) * TB] = qbuf[i].reshape(D, TB)

        buffers = (s_a, s_b)
        top = scored(parts[0], buffers[0])
        best, mass = None, None
        for n, (h, j) in enumerate(parts):
            if n + 1 == len(parts) // 2:

                @pl.when(pair == 0)
                def _():
                    k_send.wait()
                    v_send.wait()

            if n + 1 < len(parts):
                next_top = scored(parts[n + 1], buffers[(n + 1) % 2])
            now = top if best is None else jnp.maximum(best, top)
            weight = jnp.exp2(buffers[n % 2][...] - now)
            row_sum = jnp.sum(weight, axis=0, keepdims=True)
            mixture = jnp.dot(
                vt[h, :, j * CHUNK : (j + 1) * CHUNK], weight.astype(BF16),
                preferred_element_type=F32,
            )
            if best is None:
                acc[...] = mixture
                mass = row_sum
            else:
                fade = jnp.exp2(best - now)
                acc[...] = acc[...] * fade + mixture
                mass = mass * fade + row_sum
            best = now
            if n + 1 < len(parts):
                top = next_top

        answer[...] = (acc[...] * (1.0 / mass)).astype(BF16)
        logs[...] = terms(best + jnp.log2(mass))

        @pl.when(pair < NEAR)
        def _():
            for u in range(2):
                i = 2 * pair + u
                lanes = slice(u * TB, (u + 1) * TB)
                for half in range(2):
                    for part in range(SIDE):
                        first = (2 * part + half) * SLICE
                        osend[i, half, part * SLICE : (part + 1) * SLICE, :] = answer[
                            first : first + SLICE, lanes
                        ]
                    osend[i, half, HALF : HALF + STAT, :] = logs[:, lanes]
            for u in range(2):
                i = 2 * pair + u
                dy = picked([(SIDE - ORDER[n][u][0]) % SIDE for n in range(PAIRS)], pair)
                dx = picked([(SIDE - ORDER[n][u][1]) % SIDE for n in range(PAIRS)], pair)
                for half in range(2):
                    pltpu.make_async_remote_copy(
                        src_ref=osend.at[i, half], dst_ref=rbuf.at[CAP * c + core],
                        send_sem=send_sem.at[2], recv_sem=ret_sem,
                        device_id=(shifted(c, dy, dx), 2 * z + half), device_id_type=MESH,
                    ).start()

        @pl.when(pair >= NEAR)
        def _():
            for u in range(2):
                n = 2 * (pair - NEAR) + u
                lanes = slice(u * TB, (u + 1) * TB)
                for part in range(SIDE):
                    zsend[n, part, 0:WIDE, :] = answer[part * WIDE : (part + 1) * WIDE, lanes]
                    zsend[n, part, WIDE : WIDE + STAT, :] = logs[:, lanes]
            for u in range(2):
                n = 2 * (pair - NEAR) + u
                for dz in (2, 1, 3):
                    pltpu.make_async_remote_copy(
                        src_ref=zsend.at[n, lax.rem(z + dz, SIDE)], dst_ref=zbuf.at[n, z],
                        send_sem=send_sem.at[0], recv_sem=z_sem.at[n], device_id=column(dz),
                        device_id_type=MESH,
                    ).start()

        return carry

    lax.fori_loop(0, PAIRS, visit, 0)

    def settle(n):
        three = zsend.at[n, pl.ds(0, 3)]
        pltpu.make_async_copy(three, three, z_sem.at[n]).wait()
        found = [zsend[n, z]] + [zbuf[n, lax.rem(z + dz, SIDE)] for dz in range(1, SIDE)]
        total, log = joined([x[0:WIDE] for x in found], [whole(x[WIDE : WIDE + STAT]) for x in found])
        stat = terms(log)
        dy, dx = ORDER[NEAR + n // 2][n % 2]
        g = shifted(c, (SIDE - dy) % SIDE, (SIDE - dx) % SIDE)
        for half in range(2):
            fsend[2 * n + half, 0:SLICE, :] = total[half * SLICE : (half + 1) * SLICE].astype(BF16)
            fsend[2 * n + half, SLICE : SLICE + STAT, :] = stat
        for half in range(2):
            source, target = fsend.at[2 * n + half], fbuf.at[CAP * n + core]
            remote = pltpu.make_async_remote_copy(
                src_ref=source, dst_ref=target, send_sem=send_sem.at[4], recv_sem=f_sem,
                device_id=(g, 2 * z + half), device_id_type=MESH,
            )
            if dy == 0 and dx == 0:

                @pl.when(core == half)
                def _():
                    pltpu.make_async_copy(source, target, f_sem).start()

                @pl.when(core != half)
                def _():
                    remote.start()
            else:
                remote.start()

    arrived = rbuf.at[pl.ds(0, 4 * NEAR)]
    pltpu.make_async_copy(arrived, arrived, ret_sem).wait()
    for t in range(TILES):
        logs_t = [whole(rbuf[f, HALF : HALF + STAT, :]) + m for f, _, m, _ in places[t]]
        total, log = joined([rbuf[f, 0:HALF, :] for f, _, _, _ in places[t]], logs_t)
        stat = terms(log)
        for part in range(SIDE):
            xsend[part, t, 0:SLICE, :] = total[part * SLICE : (part + 1) * SLICE].astype(BF16)
            xsend[part, t, SLICE : SLICE + STAT, :] = stat
        for dz in (2, 1, 3):
            pltpu.make_async_remote_copy(
                src_ref=xsend.at[lax.rem(z + dz, SIDE), t], dst_ref=xbuf.at[z, t],
                send_sem=send_sem.at[3], recv_sem=x_sem.at[t], device_id=column(dz),
                device_id_type=MESH,
            ).start()
        xbuf[z, t] = xsend[z, t]

    for n in range(2 * FAR):
        settle(n)

    pltpu.make_async_copy(fbuf, fbuf, f_sem).wait()
    for t in range(TILES):
        three = xsend.at[pl.ds(0, 3), t]
        pltpu.make_async_copy(three, three, x_sem.at[t]).wait()
        found = [xbuf[n, t] for n in range(SIDE)]
        logs_t = [whole(x[SLICE : SLICE + STAT]) for x in found]
        for _, f, _, m in places[t]:
            found.append(fbuf[f])
            logs_t.append(whole(found[-1][SLICE : SLICE + STAT]) + m)
        total, _ = joined([x[0:SLICE] for x in found], logs_t)
        out_ref[:, t * TB : (t + 1) * TB] = total.astype(BF16)

    flat_pack = pack.at[pl.ds(0, 15)]
    pltpu.make_async_copy(flat_pack, flat_pack, pack_sem).wait()
    pltpu.make_async_copy(pack.at[0, 0], pack.at[0, 0], pack_sem).wait()
    relayed = qbuf.at[pl.ds(0, 12)]
    pltpu.make_async_copy(relayed, relayed, send_sem.at[1]).wait()
    pltpu.make_async_copy(osend, osend, send_sem.at[2]).wait()
    three = zsend.at[pl.ds(0, 3)]
    pltpu.make_async_copy(three, three, send_sem.at[0]).wait()
    pltpu.make_async_copy(xsend.at[pl.ds(0, 3)], xsend.at[pl.ds(0, 3)], send_sem.at[3]).wait()
    seven = fsend.at[pl.ds(0, 4 * FAR - 1)]
    pltpu.make_async_copy(seven, seven, send_sem.at[4]).wait()


def shards(queries, probes, key_rows, value_rows, key_scale, key_tiles):
    vmem = pl.BlockSpec(memory_space=pltpu.VMEM)
    smem = pl.BlockSpec(memory_space=pltpu.SMEM)
    hbm = pl.BlockSpec(memory_space=pl.ANY)
    dma = pltpu.SemaphoreType.DMA
    return pl.pallas_call(
        kernel,
        out_shape=jax.ShapeDtypeStruct((SLICE, TILES * TB), BF16),
        in_specs=[vmem, smem, smem, smem, hbm, hbm],
        out_specs=vmem,
        scratch_shapes=[
            pltpu.VMEM((TILES, SLICE, TB), BF16),
            pltpu.VMEM((CLUSTERS, CAP, SLICE, TB), BF16),
            pltpu.VMEM((CLUSTERS, 2 * SIDE, SLICE, TB), BF16),
            pltpu.VMEM((2, KEYS, D), BF16),
            pltpu.VMEM((KEYS, D), BF16),
            pltpu.VMEM((2, D, KEYS), BF16),
            pltpu.VMEM((2, KEYS // KB, 2 * TB), F32),
            pltpu.VMEM((2, KEYS // KB, 2 * TB), F32),
            pltpu.VMEM((2, KEYS // KB, 2 * TB), F32),
            pltpu.VMEM((D, 2 * TB), BF16),
            pltpu.VMEM((CHUNK, 2 * TB), F32),
            pltpu.VMEM((CHUNK, 2 * TB), F32),
            pltpu.VMEM((D, 2 * TB), F32),
            pltpu.VMEM((D, 2 * TB), BF16),
            pltpu.VMEM((STAT, 2 * TB), BF16),
            pltpu.VMEM((2 * NEAR, 2, HALF + STAT, TB), BF16),
            pltpu.VMEM((CAP * CLUSTERS, HALF + STAT, TB), BF16),
            pltpu.VMEM((SIDE, TILES, SLICE + STAT, TB), BF16),
            pltpu.VMEM((SIDE, TILES, SLICE + STAT, TB), BF16),
            pltpu.VMEM((2 * FAR, SIDE, WIDE + STAT, TB), BF16),
            pltpu.VMEM((2 * FAR, SIDE, WIDE + STAT, TB), BF16),
            pltpu.VMEM((4 * FAR, SLICE + STAT, TB), BF16),
            pltpu.VMEM((4 * FAR, SLICE + STAT, TB), BF16),
            dma((2,)),
            dma,
            dma((5,)),
            dma((CLUSTERS,)),
            dma((CLUSTERS,)),
            dma((CLUSTERS,)),
            dma((CLUSTERS,)),
            dma((6,)),
            dma,
            dma((TILES,)),
            dma((2 * FAR,)),
            dma,
        ],
        compiler_params=pltpu.CompilerParams(
            collective_id=0, has_side_effects=True, vmem_limit_bytes=60 * 2**20
        ),
    )(queries.T, probes, key_scale, key_tiles, key_rows, value_rows).T


def solution(mesh):
    return jax.shard_map(
        shards,
        mesh=mesh,
        in_specs=(
            P("cluster", "kshard"),
            P("cluster", None),
            P("cluster", "kshard", None),
            P("cluster", "kshard", None),
            P("cluster", "kshard"),
            P("cluster"),
        ),
        out_specs=P("cluster", "kshard"),
        check_vma=False,
    )
```
